32 devices in a mesh: win: 4 (over y, x), seq: 8 (over z, core).
Axes of the slice: x: 2, y: 2, z: 4, core: 2. Of those that a mesh axis runs over, the one named last changes fastest.
Arguments:
- conv_input: bfloat16 [384, 8192], P(None, ('win', 'seq')), parts along dimension 1, may hold values from -36 to 36, as said below
- near_weight: bfloat16 [5, 384, 384], P(None, 'seq'), may hold values from -0.125 to 0.125
- near_bias: float32 [384], replicated, may hold values from -3 to 3
- near_gain: float32 [384], replicated, may hold values from 0.25 to 1.75
- dilated_weight: bfloat16 [5, 384, 384], P(None, 'seq'), may hold values from -0.125 to 0.125
- dilated_bias: float32 [384], replicated, may hold values from -3 to 3
- far_gain: float32 [384], replicated, may hold values from 0.25 to 1.75
- pool_weight: bfloat16 [2, 384, 1536], P(None, None, 'seq'), may hold values from -0.21875 to 0.21875
- attn_gain: float32 [1536], replicated, may hold values from 0.25 to 1.75
- query_weight: bfloat16 [1536, 256], replicated, may hold values from -32 to 32
- key_weight: bfloat16 [1536, 256], replicated, may hold values from -1 to 1
- value_weight: bfloat16 [1536, 768], P('seq'), may hold values from -0.15625 to 0.15625
Outputs:
- attended: bfloat16 [4096, 768], P(('win', 'seq')), parts along dimension 0
The draws below stay inside these ranges and needn't reach their ends.
There are 4 independent parts, one for each index of `win`. The reference program is written for one: setup_inputs(seed, part) draws one part's arguments, and reference() takes and returns one part's arrays. A program takes and returns all parts, laid end to end along the dimension named above; an argument that names none is the same for every part. Nothing has to cross between parts.
Inputs may be any that keep to these rules, and one draw needn't show every extreme that they name: `conv_input`: features of the window; channels and positions have their own scales.
All inputs are finite; a program needn't handle non-finite values.
Results may differ from the reference program's by a relative error of at most 0.02.
Values may be sent and summed in bfloat16 or wider, within the bound.
A program may use at most 64 MiB of HBM per device.

```python
import math
import jax
import jax.numpy as jnp
from jax import lax

C = 384
D = 1536
HEADS = 4
KEY = 64
VAL = 192
KS = 5
DILATION_STEP = 16
POSITIONS = 1024
CONV_LEN = 2048


def draw_conv_input(key, part):
    key_base, key_chan, key_spot = jax.random.split(key, 3)
    chan = jnp.exp(jax.random.uniform(key_chan, (C, 1), jnp.float32, math.log(0.3), math.log(3.0)))
    spot = jnp.exp(jax.random.uniform(key_spot, (1, CONV_LEN), jnp.float32, math.log(0.3), math.log(3.0)))
    base = jax.random.truncated_normal(key_base, -4.0, 4.0, (C, CONV_LEN), jnp.float32)
    return (base * chan * spot).astype(jnp.bfloat16)


def weight_pair(key):
    key_query = jax.random.fold_in(key, 101)
    key_key = jax.random.fold_in(key, 102)
    scale = D ** (-0.5)
    key_part = jax.random.truncated_normal(key_key, -4.0, 4.0, (D, HEADS * KEY), jnp.float32) * scale
    noise = jax.random.truncated_normal(key_query, -4.0, 4.0, (D, HEADS * KEY), jnp.float32) * scale
    query_part = 3.0 * noise
    return (query_part, key_part)


def draw_query_weight(key, part):
    return weight_pair(key)[0].astype(jnp.bfloat16)


def draw_key_weight(key, part):
    return weight_pair(key)[1].astype(jnp.bfloat16)


def block_levels(rng, shape, cuts, low, high):
    loudness = 1.0
    for dim, shards_of in cuts:
        draws = jax.random.uniform(jax.random.fold_in(jax.random.fold_in(rng, 6), dim), (shards_of,), jnp.float32, low / len(cuts), high / len(cuts))
        loudness = loudness * jnp.repeat(jnp.exp(draws), shape[dim] // shards_of).reshape((-1,) + (1,) * (len(shape) - 1 - dim))
    return loudness


def gaussian(stream_key, extent, width, most, pieces=(), kind=jnp.bfloat16):
    values = jax.random.normal(stream_key, extent, jnp.float32) * width
    if len(pieces) > 0:
        values = block_levels(stream_key, extent, pieces, -0.22, 0.18) * values
    return jnp.clip(values, min=-most, max=most).astype(kind)


def setup_inputs(seed: int = 0, part: int = 0) -> dict:
    streams_of = jax.random.split(jax.random.key(seed), 13)
    own_keys = jax.random.split(jax.random.fold_in(streams_of[12], part), 13)
    return {
        "conv_input": draw_conv_input(jax.random.fold_in(jax.random.fold_in(streams_of[12], part), 71), part),
        "near_weight": gaussian(streams_of[1], (KS, C, C), (KS * C) ** -0.5, 0.125, ((1, 8),)),
        "near_bias": gaussian(streams_of[2], (C,), 0.5, 3.0, (), jnp.float32),
        "near_gain": jnp.clip(1.0 + 0.15 * jax.random.normal(streams_of[3], (C,), jnp.float32), 0.25, 1.75),
        "dilated_weight": gaussian(streams_of[4], (KS, C, C), (KS * C) ** -0.5, 0.125, ((1, 8),)),
        "dilated_bias": gaussian(streams_of[5], (C,), 0.5, 3.0, (), jnp.float32),
        "far_gain": jnp.clip(1.0 + 0.15 * jax.random.normal(streams_of[6], (C,), jnp.float32), 0.25, 1.75),
        "pool_weight": gaussian(streams_of[7], (2, C, D), (2 * C) ** -0.5, 0.21875, ((2, 8),)),
        "attn_gain": jnp.clip(1.0 + 0.15 * jax.random.normal(streams_of[8], (D,), jnp.float32), 0.25, 1.75),
        "query_weight": draw_query_weight(jax.random.fold_in(streams_of[12], 71), part),
        "key_weight": draw_key_weight(jax.random.fold_in(streams_of[12], 71), part),
        "value_weight": gaussian(streams_of[11], (D, HEADS * VAL), D ** -0.5, 0.15625, ((0, 8),)),
    }


def activate(field, gain):
    wide = field.astype(jnp.float32)
    square = lax.optimization_barrier(jnp.mean(wide * wide, axis=0, keepdims=True))
    scaled = wide * lax.rsqrt(square + 1e-06) * gain[:, None]
    return jax.nn.gelu(scaled, approximate=False).astype(jnp.bfloat16)

def apply_convolution(field, weight, spread):
    length = field.shape[1]
    padded = jnp.pad(field.astype(jnp.float32), ((0, 0), (2 * spread, 2 * spread)))
    stacked = jnp.stack([padded[:, t * spread:t * spread + length] for t in range(KS)])
    return jnp.einsum('toc,tcl->ol', weight.astype(jnp.float32), stacked)

def reference(conv_input, near_weight, near_bias, near_gain, dilated_weight, dilated_bias, far_gain, pool_weight, attn_gain, query_weight, key_weight, value_weight):
    near_act = activate(conv_input, near_gain)
    local_output = (conv_input.astype(jnp.float32) + near_bias[:, None] + apply_convolution(near_act, near_weight, 1)).astype(jnp.bfloat16)
    dilated_activation = activate(local_output, far_gain)
    dilated_output = (local_output.astype(jnp.float32) + dilated_bias[:, None] + apply_convolution(dilated_activation, dilated_weight, DILATION_STEP)).astype(jnp.bfloat16)
    pool_act = jax.nn.gelu(dilated_output.astype(jnp.float32), approximate=False).astype(jnp.bfloat16)
    even = pool_act[:, 0::2].astype(jnp.float32)
    odd = pool_act[:, 1::2].astype(jnp.float32)
    pooled = jnp.einsum('cp,cd->pd', even, pool_weight[0].astype(jnp.float32)) + jnp.einsum('cp,cd->pd', odd, pool_weight[1].astype(jnp.float32))
    square = lax.optimization_barrier(jnp.mean(pooled * pooled, axis=1, keepdims=True))
    normed = (pooled * lax.rsqrt(square + 1e-06) * attn_gain[None, :]).astype(jnp.bfloat16)
    queries = (jnp.dot(normed, query_weight, preferred_element_type=jnp.float32) * KEY ** (-0.5)).astype(jnp.bfloat16)
    keys = jnp.dot(normed, key_weight, preferred_element_type=jnp.float32).astype(jnp.bfloat16)
    values = jnp.dot(normed, value_weight, preferred_element_type=jnp.float32).astype(jnp.bfloat16)
    key_heads = keys.reshape(POSITIONS, HEADS, KEY).astype(jnp.float32)
    value_heads = values.reshape(POSITIONS, HEADS, VAL).astype(jnp.float32)
    block_rows = min(512, POSITIONS)
    query_blocks = queries.reshape(POSITIONS // block_rows, block_rows, HEADS, KEY)

    def one_block(query_block):
        scores = jnp.einsum('phk,nhk->hpn', query_block.astype(jnp.float32), key_heads)
        top = lax.optimization_barrier(jnp.max(scores, axis=-1, keepdims=True))
        raised = jnp.exp(scores - top)
        denom = lax.optimization_barrier(jnp.sum(raised, axis=-1))
        weights = raised.astype(jnp.bfloat16).astype(jnp.float32)
        summed = jnp.einsum('hpn,nhv->phv', weights, value_heads)
        result = summed / jnp.transpose(denom)[:, :, None]
        return result.reshape(block_rows, HEADS * VAL).astype(jnp.bfloat16)
    attended = lax.map(one_block, query_blocks)
    return attended.reshape(POSITIONS, HEADS * VAL)
```

```python
import functools

import jax
import jax.numpy as jnp
from jax import lax
from jax.experimental import pallas as pl
from jax.experimental.pallas import tpu as pltpu
from jax.sharding import PartitionSpec as P

HEADS = 4
KEY = 64
VAL = 192
KS = 5
DILATION_STEP = 16


def padded_2(block, sides, width):
    for axis, dim in sides:
        count = lax.axis_size(axis)
        forward = [(i, i + 1) for i in range(count - 1)]
        backward = [(target, source) for source, target in forward]
        low = lax.ppermute(
            lax.slice_in_dim(block, block.shape[dim] - width, None, axis=dim), axis, forward
        )
        high = lax.ppermute(lax.slice_in_dim(block, 0, width, axis=dim), axis, backward)
        block = jnp.concatenate([low, block, high], axis=dim)
    return block


def activate(field, gain):
    wide = field.astype(jnp.float32)
    square = jnp.mean(wide * wide, axis=0, keepdims=True)
    scaled = wide * lax.rsqrt(square + 1e-06) * gain[:, None]
    return jax.nn.gelu(scaled, approximate=False).astype(jnp.bfloat16)


def convolution_taps(padded, weight, spread):
    length = padded.shape[1] - 4 * spread
    stacked = jnp.stack([padded[:, t * spread : t * spread + length] for t in range(KS)])
    return jnp.einsum("toc,tcl->ol", weight, stacked, preferred_element_type=jnp.float32)


def attend_step(carry, pieces, queries, heads):
    running_top, running_sum, running_acc = carry
    keys, values = pieces
    count = keys.shape[0]
    key_heads = keys.reshape(count, heads, -1)
    value_heads = values.reshape(count, heads, -1)
    value_size = value_heads.shape[2]
    scores = jnp.einsum("phk,nhk->hpn", queries, key_heads, preferred_element_type=jnp.float32)
    new_top = jnp.maximum(running_top, jnp.max(scores, axis=-1))
    factor = jnp.exp(running_top - new_top)
    raised = jnp.exp(scores - new_top[:, :, None])
    new_sum = jnp.sum(raised, axis=-1)
    summed = jnp.einsum(
        "hpn,nhv->phv", raised.astype(jnp.bfloat16), value_heads, preferred_element_type=jnp.float32
    )
    widened = jnp.repeat(jnp.transpose(factor), value_size, axis=1)
    new_acc = running_acc * widened + summed.reshape(summed.shape[0], heads * value_size)
    return (new_top, new_sum, new_acc)


def shards(
    conv_input,
    near_weight,
    near_bias,
    near_gain,
    dilated_weight,
    dilated_bias,
    far_gain,
    pool_weight,
    attn_gain,
    query_weight,
    key_weight,
    value_weight,
):
    near_taps, dilated_taps, pool_taps = (
        lax.all_gather(near_weight, "seq", axis=1, tiled=True),
        lax.all_gather(dilated_weight, "seq", axis=1, tiled=True),
        lax.all_gather(pool_weight, "seq", axis=2, tiled=True),
    )
    near_act = activate(conv_input, near_gain)
    near_pad = padded_2(near_act, (("seq", 1),), 2)
    local_output = (
        conv_input.astype(jnp.float32)
        + near_bias[:, None]
        + convolution_taps(near_pad, near_taps, 1)
    ).astype(jnp.bfloat16)
    dilated_activation = activate(local_output, far_gain)
    dilated_padding = padded_2(dilated_activation, (("seq", 1),), 2 * DILATION_STEP)
    dilated_output = (
        local_output.astype(jnp.float32)
        + dilated_bias[:, None]
        + convolution_taps(dilated_padding, dilated_taps, DILATION_STEP)
    ).astype(jnp.bfloat16)
    pool_act = jax.nn.gelu(dilated_output.astype(jnp.float32), approximate=False).astype(
        jnp.bfloat16
    )
    pooled = jnp.einsum(
        "cp,cd->pd", pool_act[:, 0::2], pool_taps[0], preferred_element_type=jnp.float32
    )
    pooled = pooled + jnp.einsum(
        "cp,cd->pd", pool_act[:, 1::2], pool_taps[1], preferred_element_type=jnp.float32
    )
    square = jnp.mean(pooled * pooled, axis=1, keepdims=True)
    normed = (pooled * lax.rsqrt(square + 1e-06) * attn_gain[None, :]).astype(jnp.bfloat16)
    queries = (
        jnp.dot(normed, query_weight, preferred_element_type=jnp.float32) * KEY ** (-0.5)
    ).astype(jnp.bfloat16)
    keys = jnp.dot(normed, key_weight, preferred_element_type=jnp.float32).astype(jnp.bfloat16)
    rows = normed.shape[0]
    values = jnp.dot(
        normed,
        lax.all_gather(value_weight, "seq", axis=0, tiled=True),
        preferred_element_type=jnp.float32,
    ).astype(jnp.bfloat16)
    query_heads = queries.reshape(rows, HEADS, KEY)
    start_carry = (
        jnp.full((HEADS, rows), -1e30, jnp.float32),
        jnp.zeros((HEADS, rows), jnp.float32),
        jnp.zeros((rows, HEADS * VAL), jnp.float32),
    )
    final = attend_step(
        start_carry,
        (
            lax.all_gather(keys, "seq", axis=0, tiled=True),
            lax.all_gather(values, "seq", axis=0, tiled=True),
        ),
        query_heads,
        HEADS,
    )
    final_top, final_sum, final_acc = final
    denom = jnp.repeat(jnp.transpose(final_sum), VAL, axis=1)
    return (final_acc / denom).astype(jnp.bfloat16)

def fused_body(
    nz,
    x_ref,
    near_ref,
    dil_ref,
    pool_ref,
    val_ref,
    chan_ref,
    gain_ref,
    qw_ref,
    kw_ref,
    out_ref,
    x_s,
    g_near,
    g_dil,
    g_pool,
    g_val,
    g_k,
    g_v,
    taps_s,
    pooled_s,
    ssem,
    rsem,
    lsem,
):
    n = 2 * nz
    w = lax.axis_index("win")
    s0 = lax.axis_index("seq")
    z = s0 // 2
    c = s0 % 2
    wx = w + 1 - 2 * (w % 2)
    wy = w + 2 - 4 * (w // 2)
    wg = wy + 1 - 2 * (w % 2)
    partner = s0 + 1 - 2 * c
    cross = s0 - 1 + 2 * c
    cross_ok = jnp.logical_and(cross >= 0, cross < n)
    local = x_ref.shape[1]
    ups = {"u": z + 1 < nz, "d": z > 0}
    steps = [(way, d) for d in range(1, nz) for way in ("u", "d")]

    def exists(way, d):
        return z >= d if way == "u" else z + d < nz

    def shard_of(way, d, core):
        return 2 * (z - d if way == "u" else z + d) + core

    def onward(way):
        return {"win": w, "seq": s0 + 2 if way == "u" else s0 - 2}

    to_x = {"win": wx, "seq": s0}
    to_y = {"win": wy, "seq": s0}
    to_c = {"win": w, "seq": partner}

    table = {}
    pending = []

    def remote(label, src, dst, device):
        index = table.setdefault(label, len(table))
        return pltpu.make_async_remote_copy(
            src_ref=src,
            dst_ref=dst,
            send_sem=ssem.at[index],
            recv_sem=rsem.at[index],
            device_id=device,
            device_id_type=pl.DeviceIdType.MESH,
        )

    def send(cond, label, src, dst, device):
        def go():
            remote(label, src(), dst(), device).start()

        def end():
            remote(label, src(), dst(), device).wait_send()

        if cond is None:
            go()
        else:
            pl.when(cond)(go)
        pending.append((cond, end))

    def receive(label, dst):
        remote(label, dst, dst, to_c).wait_recv()

    sources = {"A": near_ref, "B": dil_ref, "C": pool_ref, "D": val_ref}
    held = {"A": g_near, "B": g_dil, "C": g_pool, "D": g_val, "K": g_k, "V": g_v}
    by_x = {"A": True, "B": False, "C": True, "D": False}

    def part(ref, q):
        rows = ref.shape[0] // 4
        return ref.at[pl.ds(pl.multiple_of(q * rows, 16), rows)]

    def region(p, s, q):
        rows = held[p].shape[1] // 4
        return held[p].at[s, pl.ds(pl.multiple_of(q * rows, 16), rows)]

    def local_copy(p):
        return pltpu.make_async_copy(sources[p], held[p].at[s0], lsem.at["ABCD".index(p)])

    def begin(p):
        for way in ("u", "d"):
            send(
                ups[way],
                (p, "z", way, 1),
                lambda: part(sources[p], w),
                lambda: region(p, s0, w),
                onward(way),
            )

    def begin_core(p):
        local_copy(p).start()
        send(None, (p, "c"), lambda: sources[p], lambda: held[p].at[s0], to_c)

    def step1(p):
        for way, d in steps:
            s = shard_of(way, d, c)
            piece = lambda s=s: region(p, s, w)
            ok = exists(way, d)
            pl.when(ok)(lambda: receive((p, "z", way, d), piece()))
            if d + 1 < nz:
                more = jnp.logical_and(ok, ups[way])
                send(more, (p, "z", way, d + 1), piece, piece, onward(way))
            send(ok, (p, "x", way, d), piece, piece, to_x)
            send(ok, (p, "y", way, d), piece, piece, to_y)

    def step2(p):
        for way, d in steps:
            s = shard_of(way, d, c)
            ok = exists(way, d)

            @pl.when(ok)
            def _():
                receive((p, "x", way, d), region(p, s, wx))
                receive((p, "y", way, d), region(p, s, wy))

            q, device = (wy, to_x) if by_x[p] else (wx, to_y)
            piece = lambda s=s, q=q: region(p, s, q)
            send(ok, (p, "g", way, d), piece, piece, device)

    def step3(p):
        for way, d in steps:
            s = shard_of(way, d, c)
            ok = exists(way, d)
            pl.when(ok)(lambda: receive((p, "g", way, d), region(p, s, wg)))
            whole = lambda s=s: held[p].at[s]
            send(ok, (p, "c", way, d), whole, whole, to_c)

    def step4(p):
        if p in sources:
            local_copy(p).wait()
        receive((p, "c"), held[p].at[partner])
        for way, d in steps:
            s = shard_of(way, d, 1 - c)
            pl.when(exists(way, d))(lambda: receive((p, "c", way, d), held[p].at[s]))

    def begin_line(p):
        mine = lambda: held[p].at[s0]
        for way in ("u", "d"):
            send(ups[way], (p, "z", way, 1), mine, mine, onward(way))
        send(None, (p, "c"), mine, mine, to_c)

    def line(p):
        for way, d in steps:
            s = shard_of(way, d, c)
            whole = lambda s=s: held[p].at[s]
            ok = exists(way, d)
            pl.when(ok)(lambda: receive((p, "z", way, d), whole()))
            if d + 1 < nz:
                more = jnp.logical_and(ok, ups[way])
                send(more, (p, "z", way, d + 1), whole, whole, onward(way))
            send(ok, (p, "c", way, d), whole, whole, to_c)

    barrier = pltpu.get_barrier_semaphore()

    def greet(device):
        pl.semaphore_signal(
            barrier, inc=1, device_id=device, device_id_type=pl.DeviceIdType.MESH
        )

    for device in (to_x, to_y, to_c):
        greet(device)
    for cond, device in (
        (ups["u"], onward("u")),
        (ups["d"], onward("d")),
        (cross_ok, {"win": w, "seq": cross}),
    ):
        pl.when(cond)(lambda: greet(device))
    above, below = 1 - (z + 1) // nz, 1 - (nz - z) // nz
    pl.semaphore_wait(barrier, 3 + above + below + c * above + (1 - c) * below)

    begin("A")
    right_ok, left_ok = s0 + 1 < n, s0 > 0
    send(
        right_ok,
        "to right",
        lambda: x_ref.at[:, pl.ds(local - 128, 128)],
        lambda: x_s.at[:, pl.ds(0, 128)],
        {"win": w, "seq": s0 + 1},
    )
    send(
        left_ok,
        "to left",
        lambda: x_ref.at[:, pl.ds(0, 128)],
        lambda: x_s.at[:, pl.ds(128 + local, 128)],
        {"win": w, "seq": s0 - 1},
    )
    own_x = pltpu.make_async_copy(x_ref, x_s.at[:, pl.ds(128, local)], lsem.at[4])
    own_x.start()
    begin_core("A")
    for p in "BCD":
        begin(p)
        begin_core(p)
    own_x.wait()
    pl.when(left_ok)(lambda: receive("to right", x_s.at[:, pl.ds(0, 128)]))
    pl.when(right_ok)(lambda: receive("to left", x_s.at[:, pl.ds(128 + local, 128)]))

    wide = local + 128
    place = s0 * local - 64 + lax.broadcasted_iota(jnp.int32, (1, wide), 1)
    inside = jnp.logical_and(place >= 0, place < n * local)

    def act(field, gain):
        square = jnp.mean(field * field, axis=0, keepdims=True)
        scaled = field * lax.rsqrt(square + 1e-06) * gain
        return gelu(scaled)

    def conv(stack, length, weights):
        total = None
        for t in range(KS):
            taps = weights[:, pl.ds(t * rows, rows), :].reshape(channels, channels)
            term = jnp.dot(
                taps, stack[t, :, pl.ds(0, length)], preferred_element_type=jnp.float32
            )
            total = term if total is None else total + term
        return total

    channels = x_ref.shape[0]
    rows = channels // n
    x = pltpu.roll(x_s[...].astype(jnp.float32), wide + 64, 1)[:, :wide]
    x = jnp.where(inside, x, 0.0)
    near_act = act(x, chan_ref[:, 1:2])
    for t in range(KS):
        shift = (2 - t) % wide
        rolled = near_act if shift == 0 else pltpu.roll(near_act, shift, 1)
        taps_s[t] = rolled.astype(jnp.bfloat16)
    step1("A")
    step2("A")
    step3("A")
    step1("B")
    step4("A")
    near_out = (x + chan_ref[:, 0:1] + conv(taps_s, wide, g_near)).astype(jnp.bfloat16)
    step2("B")
    near_wide = near_out.astype(jnp.float32)
    far_act = jnp.where(inside, act(near_wide, chan_ref[:, 3:4]), 0.0)
    step3("B")
    step1("C")
    for t in range(KS):
        rolled = pltpu.roll(far_act, wide - 64 - DILATION_STEP * (t - 2), 1)
        taps_s[t, :, pl.ds(0, local)] = rolled[:, :local].astype(jnp.bfloat16)
    own_out = pltpu.roll(near_wide, wide - 64, 1)[:, :local]
    step2("C")
    step4("B")
    far_out = (own_out + chan_ref[:, 2:3] + conv(taps_s, local, g_dil)).astype(jnp.bfloat16)
    step3("C")
    step1("D")
    pool_act = gelu(far_out.astype(jnp.float32)).astype(jnp.bfloat16)
    half = local // 2
    row = lax.broadcasted_iota(jnp.int32, (local, local), 0)
    col = lax.broadcasted_iota(jnp.int32, (local, local), 1)
    picker = jnp.where(row < half, 2 * row, 2 * (row - half) + 1) == col
    picked = lax.dot_general(
        picker.astype(jnp.bfloat16),
        pool_act,
        (((1,), (1,)), ((), ())),
        preferred_element_type=jnp.float32,
    ).astype(jnp.bfloat16)
    even, odd = picked[:half], picked[half:]
    step2("D")
    step4("C")
    square = None
    for j in range(n):
        chunk = jnp.dot(
            even, g_pool[j, pl.ds(0, channels), :], preferred_element_type=jnp.float32
        ) + jnp.dot(
            odd, g_pool[j, pl.ds(channels, channels), :], preferred_element_type=jnp.float32
        )
        pooled_s[j] = chunk
        term = jnp.sum(chunk * chunk, axis=1, keepdims=True)
        square = term if square is None else square + term
    step3("D")
    depth = pooled_s.shape[2]
    scale = lax.rsqrt(square / (n * depth) + 1e-06)
    normed = [
        (pooled_s[j] * scale * gain_ref[j]).astype(jnp.bfloat16) for j in range(n)
    ]

    def project(weight):
        total = None
        for j in range(n):
            term = jnp.dot(normed[j], weight(j), preferred_element_type=jnp.float32)
            total = term if total is None else total + term
        return total

    keys = project(lambda j: kw_ref[pl.ds(j * depth, depth), :])
    g_k[s0] = keys.astype(jnp.bfloat16)
    begin_line("K")
    step4("D")
    values = project(lambda j: g_val[j])
    g_v[s0] = values.astype(jnp.bfloat16)
    begin_line("V")
    line("K")
    queries = project(lambda j: qw_ref[pl.ds(j * depth, depth), :]) * KEY ** (-0.5)
    queries = queries.astype(jnp.bfloat16)
    step4("K")
    lane = lax.broadcasted_iota(jnp.int32, (half, 2 * KEY), 1)
    weights, sums = [], []
    for pair in range(HEADS // 2):
        side = queries[:, pair * 2 * KEY : (pair + 1) * 2 * KEY]
        both = jnp.concatenate(
            [jnp.where(lane < KEY, side, 0.0), jnp.where(lane < KEY, 0.0, side)], axis=0
        ).astype(jnp.bfloat16)
        scores = lax.dot_general(
            both,
            g_k[:, :, pl.ds(pair * 2 * KEY, 2 * KEY)].reshape(n * half, 2 * KEY),
            (((1,), (1,)), ((), ())),
            preferred_element_type=jnp.float32,
        )
        raised = jnp.exp(scores - jnp.max(scores, axis=1, keepdims=True))
        sums.append(jnp.sum(raised, axis=1, keepdims=True))
        weights.append(raised.astype(jnp.bfloat16))
        if pair == 0:
            line("V")
    step4("V")
    lane = lax.broadcasted_iota(jnp.int32, (half, 2 * VAL), 1)
    for pair in range(HEADS // 2):
        span = pl.ds(pair * 2 * VAL, 2 * VAL)
        summed = jnp.dot(
            weights[pair],
            g_v[:, :, span].reshape(n * half, 2 * VAL),
            preferred_element_type=jnp.float32,
        )
        result = summed / sums[pair]
        out_ref[:, span] = jnp.where(lane < VAL, result[:half], result[half:]).astype(
            jnp.bfloat16
        )
    for cond, end in pending:
        if cond is None:
            end()
        else:
            pl.when(cond)(end)


def gelu(x):
    return 0.5 * x * (1.0 + lax.erf(x * 0.7071067811865476))


def fused(
    conv_input,
    near_weight,
    near_bias,
    near_gain,
    dilated_weight,
    dilated_bias,
    far_gain,
    pool_weight,
    attn_gain,
    query_weight,
    key_weight,
    value_weight,
):
    n = lax.axis_size("seq")
    nz = n // 2
    channels, local = conv_input.shape
    half = local // 2

    def flat(weight):
        rows = weight.shape[0] * weight.shape[1]
        weight = weight.reshape(rows, channels)
        return jnp.pad(weight, ((0, -rows % 64), (0, 0)))

    near, dilated = flat(near_weight), flat(dilated_weight)
    depth = pool_weight.shape[2]
    pool = pool_weight.reshape(2 * channels, depth)
    chan = jnp.stack([near_bias, near_gain, dilated_bias, far_gain], axis=1)
    gain = attn_gain.reshape(n, 1, depth)
    any_spec = pl.BlockSpec(memory_space=pl.ANY)
    vmem = pl.BlockSpec(memory_space=pltpu.VMEM)
    count = (4 * 5 + 2 * 2) * 2 * (nz - 1) + 6 + 2
    gathered = lambda a: pltpu.VMEM((n,) + a.shape, jnp.bfloat16)
    wide = local + 128
    return pl.pallas_call(
        functools.partial(fused_body, nz),
        out_shape=jax.ShapeDtypeStruct((half, HEADS * VAL), jnp.bfloat16),
        in_specs=[any_spec] * 5 + [vmem] * 4,
        out_specs=vmem,
        scratch_shapes=[
            pltpu.VMEM((channels, local + 256), jnp.bfloat16),
            gathered(near),
            gathered(dilated),
            gathered(pool),
            gathered(value_weight),
            pltpu.VMEM((n, half, HEADS * KEY), jnp.bfloat16),
            pltpu.VMEM((n, half, HEADS * VAL), jnp.bfloat16),
            pltpu.VMEM((KS, channels, wide), jnp.bfloat16),
            pltpu.VMEM((n, half, depth), jnp.float32),
            pltpu.SemaphoreType.DMA((count,)),
            pltpu.SemaphoreType.DMA((count,)),
            pltpu.SemaphoreType.DMA((5,)),
        ],
        compiler_params=pltpu.CompilerParams(collective_id=0, has_side_effects=True),
    )(
        conv_input,
        near,
        dilated,
        pool,
        value_weight,
        chan,
        gain,
        query_weight,
        key_weight,
    )


def solution(mesh):
    placed = (
        P(None, ("win", "seq")),
        P(None, "seq", None),
        P(),
        P(),
        P(None, "seq", None),
        P(),
        P(),
        P(None, None, "seq"),
        P(),
        P(),
        P(),
        P("seq", None),
    )

    def body(*args):
        near_weight, value_weight = args[1], args[11]
        count = lax.axis_size("seq")
        fits = (
            lax.axis_size("win") == 4
            and count % 2 == 0
            and near_weight.shape[1] % 16 == 0
            and value_weight.shape[0] % 64 == 0
            and args[0].shape[1] % 128 == 0
        )
        return fused(*args) if fits else shards(*args)

    return jax.shard_map(
        body, mesh=mesh, in_specs=placed, out_specs=P(("win", "seq"), None), check_vma=False
    )
```

```python
import functools

import jax
import jax.numpy as jnp
from jax import lax
from jax.experimental import pallas as pl
from jax.experimental.pallas import tpu as pltpu
from jax.sharding import PartitionSpec as P

HEADS = 4
KEY = 64
VAL = 192
KS = 5
DILATION_STEP = 16


def padded_2(block, sides, width):
    for axis, dim in sides:
        count = lax.axis_size(axis)
        forward = [(i, i + 1) for i in range(count - 1)]
        backward = [(target, source) for source, target in forward]
        low = lax.ppermute(
            lax.slice_in_dim(block, block.shape[dim] - width, None, axis=dim), axis, forward
        )
        high = lax.ppermute(lax.slice_in_dim(block, 0, width, axis=dim), axis, backward)
        block = jnp.concatenate([low, block, high], axis=dim)
    return block


def activate(field, gain):
    wide = field.astype(jnp.float32)
    square = jnp.mean(wide * wide, axis=0, keepdims=True)
    scaled = wide * lax.rsqrt(square + 1e-06) * gain[:, None]
    return jax.nn.gelu(scaled, approximate=False).astype(jnp.bfloat16)


def convolution_taps(padded, weight, spread):
    length = padded.shape[1] - 4 * spread
    stacked = jnp.stack([padded[:, t * spread : t * spread + length] for t in range(KS)])
    return jnp.einsum("toc,tcl->ol", weight, stacked, preferred_element_type=jnp.float32)


def attend_step(carry, pieces, queries, heads):
    running_top, running_sum, running_acc = carry
    keys, values = pieces
    count = keys.shape[0]
    key_heads = keys.reshape(count, heads, -1)
    value_heads = values.reshape(count, heads, -1)
    value_size = value_heads.shape[2]
    scores = jnp.einsum("phk,nhk->hpn", queries, key_heads, preferred_element_type=jnp.float32)
    new_top = jnp.maximum(running_top, jnp.max(scores, axis=-1))
    factor = jnp.exp(running_top - new_top)
    raised = jnp.exp(scores - new_top[:, :, None])
    new_sum = jnp.sum(raised, axis=-1)
    summed = jnp.einsum(
        "hpn,nhv->phv", raised.astype(jnp.bfloat16), value_heads, preferred_element_type=jnp.float32
    )
    widened = jnp.repeat(jnp.transpose(factor), value_size, axis=1)
    new_acc = running_acc * widened + summed.reshape(summed.shape[0], heads * value_size)
    return (new_top, new_sum, new_acc)


def shards(
    conv_input,
    near_weight,
    near_bias,
    near_gain,
    dilated_weight,
    dilated_bias,
    far_gain,
    pool_weight,
    attn_gain,
    query_weight,
    key_weight,
    value_weight,
):
    near_taps, dilated_taps, pool_taps = (
        lax.all_gather(near_weight, "seq", axis=1, tiled=True),
        lax.all_gather(dilated_weight, "seq", axis=1, tiled=True),
        lax.all_gather(pool_weight, "seq", axis=2, tiled=True),
    )
    near_act = activate(conv_input, near_gain)
    near_pad = padded_2(near_act, (("seq", 1),), 2)
    local_output = (
        conv_input.astype(jnp.float32)
        + near_bias[:, None]
        + convolution_taps(near_pad, near_taps, 1)
    ).astype(jnp.bfloat16)
    dilated_activation = activate(local_output, far_gain)
    dilated_padding = padded_2(dilated_activation, (("seq", 1),), 2 * DILATION_STEP)
    dilated_output = (
        local_output.astype(jnp.float32)
        + dilated_bias[:, None]
        + convolution_taps(dilated_padding, dilated_taps, DILATION_STEP)
    ).astype(jnp.bfloat16)
    pool_act = jax.nn.gelu(dilated_output.astype(jnp.float32), approximate=False).astype(
        jnp.bfloat16
    )
    pooled = jnp.einsum(
        "cp,cd->pd", pool_act[:, 0::2], pool_taps[0], preferred_element_type=jnp.float32
    )
    pooled = pooled + jnp.einsum(
        "cp,cd->pd", pool_act[:, 1::2], pool_taps[1], preferred_element_type=jnp.float32
    )
    square = jnp.mean(pooled * pooled, axis=1, keepdims=True)
    normed = (pooled * lax.rsqrt(square + 1e-06) * attn_gain[None, :]).astype(jnp.bfloat16)
    queries = (
        jnp.dot(normed, query_weight, preferred_element_type=jnp.float32) * KEY ** (-0.5)
    ).astype(jnp.bfloat16)
    keys = jnp.dot(normed, key_weight, preferred_element_type=jnp.float32).astype(jnp.bfloat16)
    rows = normed.shape[0]
    values = jnp.dot(
        normed,
        lax.all_gather(value_weight, "seq", axis=0, tiled=True),
        preferred_element_type=jnp.float32,
    ).astype(jnp.bfloat16)
    query_heads = queries.reshape(rows, HEADS, KEY)
    start_carry = (
        jnp.full((HEADS, rows), -1e30, jnp.float32),
        jnp.zeros((HEADS, rows), jnp.float32),
        jnp.zeros((rows, HEADS * VAL), jnp.float32),
    )
    final = attend_step(
        start_carry,
        (
            lax.all_gather(keys, "seq", axis=0, tiled=True),
            lax.all_gather(values, "seq", axis=0, tiled=True),
        ),
        query_heads,
        HEADS,
    )
    final_top, final_sum, final_acc = final
    denom = jnp.repeat(jnp.transpose(final_sum), VAL, axis=1)
    return (final_acc / denom).astype(jnp.bfloat16)

def fused_body(
    nz,
    x_ref,
    near_ref,
    dil_ref,
    pool_ref,
    val_ref,
    nb_ref,
    ng_ref,
    db_ref,
    fg_ref,
    gain_ref,
    qw_hbm,
    kw_hbm,
    out_ref,
    x_s,
    g_near,
    g_dil,
    g_pool,
    g_val,
    g_k,
    g_v,
    taps_s,
    qw_ref,
    kw_ref,
    ssem,
    rsem,
    lsem,
):
    n = 2 * nz
    w = lax.axis_index("win")
    s0 = lax.axis_index("seq")
    z = s0 // 2
    c = s0 % 2
    wx = w + 1 - 2 * (w % 2)
    wy = w + 2 - 4 * (w // 2)
    wg = wy + 1 - 2 * (w % 2)
    partner = s0 + 1 - 2 * c
    cross = s0 - 1 + 2 * c
    cross_ok = jnp.logical_and(cross >= 0, cross < n)
    local = x_ref.shape[1]
    ups = {"u": z + 1 < nz, "d": z > 0}
    steps = [(way, d) for d in range(1, nz) for way in ("u", "d")]

    def exists(way, d):
        return z >= d if way == "u" else z + d < nz

    def shard_of(way, d, core):
        return 2 * (z - d if way == "u" else z + d) + core

    def onward(way):
        return {"win": w, "seq": s0 + 2 if way == "u" else s0 - 2}

    to_x = {"win": wx, "seq": s0}
    to_y = {"win": wy, "seq": s0}
    to_c = {"win": w, "seq": partner}

    table = {}
    pending = []

    def remote(label, src, dst, device):
        index = table.setdefault(label, len(table))
        return pltpu.make_async_remote_copy(
            src_ref=src,
            dst_ref=dst,
            send_sem=ssem.at[index],
            recv_sem=rsem.at[index],
            device_id=device,
            device_id_type=pl.DeviceIdType.MESH,
        )

    def send(cond, label, src, dst, device):
        def go():
            remote(label, src(), dst(), device).start()

        def end():
            remote(label, src(), dst(), device).wait_send()

        if cond is None:
            go()
        else:
            pl.when(cond)(go)
        pending.append((cond, end))

    def receive(label, dst):
        remote(label, dst, dst, to_c).wait_recv()

    sources = {"A": near_ref, "B": dil_ref, "C": pool_ref, "D": val_ref}
    held = {"A": g_near, "B": g_dil, "C": g_pool, "D": g_val, "K": g_k, "V": g_v}
    by_x = {"A": True, "B": False, "C": True, "D": False}

    def solid(p, s):
        return held[p].at[s, pl.ds(0, sources[p].shape[0])]

    def region(p, s, q):
        rows = held[p].shape[1] // 4
        return held[p].at[s, pl.ds(pl.multiple_of(q * rows, 16), rows)]

    def local_copy(p):
        return pltpu.make_async_copy(sources[p], solid(p, s0), lsem.at["ABCD".index(p)])

    def begin(p):
        for way in ("u", "d"):
            send(
                ups[way],
                (p, "z", way, 1),
                lambda: region(p, s0, w),
                lambda: region(p, s0, w),
                onward(way),
            )

    def begin_core(p):
        send(None, (p, "c"), lambda: sources[p], lambda: solid(p, s0), to_c)

    def step1(p):
        for way, d in steps:
            s = shard_of(way, d, c)
            piece = lambda s=s: region(p, s, w)
            ok = exists(way, d)
            pl.when(ok)(lambda: receive((p, "z", way, d), piece()))
            if d + 1 < nz:
                more = jnp.logical_and(ok, ups[way])
                send(more, (p, "z", way, d + 1), piece, piece, onward(way))
            send(ok, (p, "x", way, d), piece, piece, to_x)
            send(ok, (p, "y", way, d), piece, piece, to_y)

    def step2(p):
        for way, d in steps:
            s = shard_of(way, d, c)
            ok = exists(way, d)

            @pl.when(ok)
            def _():
                receive((p, "x", way, d), region(p, s, wx))
                receive((p, "y", way, d), region(p, s, wy))

            q, device = (wy, to_x) if by_x[p] else (wx, to_y)
            piece = lambda s=s, q=q: region(p, s, q)
            send(ok, (p, "g", way, d), piece, piece, device)

    def step3(p):
        for way, d in steps:
            s = shard_of(way, d, c)
            ok = exists(way, d)
            pl.when(ok)(lambda: receive((p, "g", way, d), region(p, s, wg)))
            whole = lambda s=s: solid(p, s)
            send(ok, (p, "c", way, d), whole, whole, to_c)

    def step4(p):
        view = solid if p in sources else lambda p, s: held[p].at[s]
        receive((p, "c"), view(p, partner))
        for way, d in steps:
            s = shard_of(way, d, 1 - c)
            pl.when(exists(way, d))(lambda: receive((p, "c", way, d), view(p, s)))

    def begin_line(p):
        mine = lambda: held[p].at[s0]
        for way in ("u", "d"):
            send(ups[way], (p, "z", way, 1), mine, mine, onward(way))
        send(None, (p, "c"), mine, mine, to_c)

    def line(p):
        for way, d in steps:
            s = shard_of(way, d, c)
            whole = lambda s=s: held[p].at[s]
            ok = exists(way, d)
            pl.when(ok)(lambda: receive((p, "z", way, d), whole()))
            if d + 1 < nz:
                more = jnp.logical_and(ok, ups[way])
                send(more, (p, "z", way, d + 1), whole, whole, onward(way))
            send(ok, (p, "c", way, d), whole, whole, to_c)

    own_x = pltpu.make_async_copy(x_ref, x_s.at[:, pl.ds(128, local)], lsem.at[4])
    own_q = pltpu.make_async_copy(qw_hbm, qw_ref, lsem.at[5])
    own_k = pltpu.make_async_copy(kw_hbm, kw_ref, lsem.at[6])
    local_copy("A").start()
    own_x.start()
    for p in "BCD":
        local_copy(p).start()
    own_k.start()
    own_q.start()

    barrier = pltpu.get_barrier_semaphore()

    def greet(device):
        pl.semaphore_signal(
            barrier, inc=1, device_id=device, device_id_type=pl.DeviceIdType.MESH
        )

    for device in (to_x, to_y, to_c):
        greet(device)
    for cond, device in (
        (ups["u"], onward("u")),
        (ups["d"], onward("d")),
        (cross_ok, {"win": w, "seq": cross}),
    ):
        pl.when(cond)(lambda: greet(device))
    above, below = 1 - (z + 1) // nz, 1 - (nz - z) // nz
    pl.semaphore_wait(barrier, 3 + above + below + c * above + (1 - c) * below)

    local_copy("A").wait()
    begin("A")
    right_ok, left_ok = s0 + 1 < n, s0 > 0
    send(
        right_ok,
        "to right",
        lambda: x_ref.at[:, pl.ds(local - 128, 128)],
        lambda: x_s.at[:, pl.ds(0, 128)],
        {"win": w, "seq": s0 + 1},
    )
    send(
        left_ok,
        "to left",
        lambda: x_ref.at[:, pl.ds(0, 128)],
        lambda: x_s.at[:, pl.ds(128 + local, 128)],
        {"win": w, "seq": s0 - 1},
    )
    begin_core("A")
    for p in "BCD":
        local_copy(p).wait()
        begin(p)
        begin_core(p)
    own_x.wait()
    pl.when(left_ok)(lambda: receive("to right", x_s.at[:, pl.ds(0, 128)]))
    pl.when(right_ok)(lambda: receive("to left", x_s.at[:, pl.ds(128 + local, 128)]))

    wide = local + 128
    place = s0 * local - 64 + lax.broadcasted_iota(jnp.int32, (1, wide), 1)
    inside = jnp.logical_and(place >= 0, place < n * local)

    def act(field, gain):
        square = jnp.mean(field * field, axis=0, keepdims=True)
        scaled = field * lax.rsqrt(square + 1e-06) * gain
        return gelu(scaled)

    def conv(stack, length, weights):
        total = None
        for t in range(KS):
            taps = weights[:, pl.ds(t * rows, rows), :].reshape(channels, channels)
            term = jnp.dot(
                taps, stack[t, :, pl.ds(0, length)], preferred_element_type=jnp.float32
            )
            total = term if total is None else total + term
        return total

    channels = x_ref.shape[0]
    rows = channels // n
    diagonal = lax.broadcasted_iota(
        jnp.int32, (channels, channels), 0
    ) == lax.broadcasted_iota(jnp.int32, (channels, channels), 1)

    def column(ref):
        return jnp.sum(jnp.where(diagonal, ref[...].reshape(1, channels), 0.0), axis=1, keepdims=True)

    x = pltpu.roll(x_s[...].astype(jnp.float32), wide + 64, 1)[:, :wide]
    x = jnp.where(inside, x, 0.0)
    near_act = act(x, column(ng_ref))
    for t in range(KS):
        shift = (2 - t) % wide
        rolled = near_act if shift == 0 else pltpu.roll(near_act, shift, 1)
        taps_s[t] = rolled.astype(jnp.bfloat16)
    step1("A")
    step2("A")
    step1("B")
    step3("A")
    step2("B")
    step1("C")
    step4("A")
    near_out = (x + column(nb_ref) + conv(taps_s, wide, g_near)).astype(jnp.bfloat16)
    step3("B")
    step2("C")
    near_wide = near_out.astype(jnp.float32)
    far_act = jnp.where(inside, act(near_wide, column(fg_ref)), 0.0)
    step1("D")
    for t in range(KS):
        rolled = pltpu.roll(far_act, wide - 64 - DILATION_STEP * (t - 2), 1)
        taps_s[t, :, pl.ds(0, local)] = rolled[:, :local].astype(jnp.bfloat16)
    own_out = pltpu.roll(near_wide, wide - 64, 1)[:, :local]
    step4("B")
    step3("C")
    far_out = (own_out + column(db_ref) + conv(taps_s, local, g_dil)).astype(jnp.bfloat16)
    step2("D")
    pool_act = gelu(far_out.astype(jnp.float32)).astype(jnp.bfloat16)
    half = local // 2
    row = lax.broadcasted_iota(jnp.int32, (local, local), 0)
    col = lax.broadcasted_iota(jnp.int32, (local, local), 1)
    picker = jnp.where(row < half, 2 * row, 2 * (row - half) + 1) == col
    picked = lax.dot_general(
        picker.astype(jnp.bfloat16),
        pool_act,
        (((1,), (1,)), ((), ())),
        preferred_element_type=jnp.float32,
    ).astype(jnp.bfloat16)
    even, odd = picked[:half], picked[half:]
    step4("C")
    depth = pool_ref.shape[0] // 2
    features = n * depth

    def pool(rows_of, tap):
        taps = g_pool[:, pl.ds(tap * depth, depth), :].reshape(features, channels)
        return lax.dot_general(
            rows_of, taps, (((1,), (1,)), ((), ())), preferred_element_type=jnp.float32
        )

    pooled = pool(even, 0) + pool(odd, 1)
    square = jnp.mean(pooled * pooled, axis=1, keepdims=True)
    gain = gain_ref[...].reshape(1, features)
    normed = (pooled * lax.rsqrt(square + 1e-06) * gain).astype(jnp.bfloat16)
    step3("D")
    own_k.wait()
    own_q.wait()

    def project(weight):
        return jnp.dot(normed, weight, preferred_element_type=jnp.float32)

    keys = project(kw_ref[...])
    g_k[s0] = keys.astype(jnp.bfloat16)
    begin_line("K")
    step4("D")
    values = project(g_val[...].reshape(features, HEADS * VAL))
    g_v[s0] = values.astype(jnp.bfloat16)
    begin_line("V")
    line("K")
    queries = project(qw_ref[...]) * KEY ** (-0.5)
    queries = queries.astype(jnp.bfloat16)
    step4("K")
    lane = lax.broadcasted_iota(jnp.int32, (half, 2 * KEY), 1)
    weights, sums = [], []
    for pair in range(HEADS // 2):
        side = queries[:, pair * 2 * KEY : (pair + 1) * 2 * KEY]
        both = jnp.concatenate(
            [jnp.where(lane < KEY, side, 0.0), jnp.where(lane < KEY, 0.0, side)], axis=0
        ).astype(jnp.bfloat16)
        scores = lax.dot_general(
            both,
            g_k[:, :, pl.ds(pair * 2 * KEY, 2 * KEY)].reshape(n * half, 2 * KEY),
            (((1,), (1,)), ((), ())),
            preferred_element_type=jnp.float32,
        )
        raised = jnp.exp(scores - jnp.max(scores, axis=1, keepdims=True))
        sums.append(jnp.sum(raised, axis=1, keepdims=True))
        weights.append(raised.astype(jnp.bfloat16))
        if pair == 0:
            line("V")
    step4("V")
    lane = lax.broadcasted_iota(jnp.int32, (half, 2 * VAL), 1)
    for pair in range(HEADS // 2):
        span = pl.ds(pair * 2 * VAL, 2 * VAL)
        summed = jnp.dot(
            weights[pair],
            g_v[:, :, span].reshape(n * half, 2 * VAL),
            preferred_element_type=jnp.float32,
        )
        result = summed / sums[pair]
        out_ref[:, span] = jnp.where(lane < VAL, result[:half], result[half:]).astype(
            jnp.bfloat16
        )
    for cond, end in pending:
        if cond is None:
            end()
        else:
            pl.when(cond)(end)


def gelu(x):
    return 0.5 * x * (1.0 + lax.erf(x * 0.7071067811865476))


def fused(
    conv_input,
    near_weight,
    near_bias,
    near_gain,
    dilated_weight,
    dilated_bias,
    far_gain,
    pool_weight,
    attn_gain,
    query_weight,
    key_weight,
    value_weight,
):
    n = lax.axis_size("seq")
    nz = n // 2
    channels, local = conv_input.shape
    half = local // 2

    def flat(weight):
        return weight.reshape(weight.shape[0] * weight.shape[1], channels)

    near, dilated = flat(near_weight), flat(dilated_weight)
    pool = flat(jnp.transpose(pool_weight, (0, 2, 1)))
    any_spec = pl.BlockSpec(memory_space=pl.ANY)
    vmem = pl.BlockSpec(memory_space=pltpu.VMEM)
    count = (4 * 5 + 2 * 2) * 2 * (nz - 1) + 6 + 2
    gathered = lambda a: pltpu.VMEM((n, a.shape[0] + -a.shape[0] % 64, a.shape[1]), jnp.bfloat16)
    wide = local + 128
    return pl.pallas_call(
        functools.partial(fused_body, nz),
        out_shape=jax.ShapeDtypeStruct((half, HEADS * VAL), jnp.bfloat16),
        in_specs=[any_spec] * 5 + [vmem] * 5 + [any_spec] * 2,
        out_specs=vmem,
        scratch_shapes=[
            pltpu.VMEM((channels, local + 256), jnp.bfloat16),
            gathered(near),
            gathered(dilated),
            gathered(pool),
            gathered(value_weight),
            pltpu.VMEM((n, half, HEADS * KEY), jnp.bfloat16),
            pltpu.VMEM((n, half, HEADS * VAL), jnp.bfloat16),
            pltpu.VMEM((KS, channels, wide), jnp.bfloat16),
            pltpu.VMEM(query_weight.shape, jnp.bfloat16),
            pltpu.VMEM(key_weight.shape, jnp.bfloat16),
            pltpu.SemaphoreType.DMA((count,)),
            pltpu.SemaphoreType.DMA((count,)),
            pltpu.SemaphoreType.DMA((7,)),
        ],
        compiler_params=pltpu.CompilerParams(collective_id=0, has_side_effects=True),
    )(
        conv_input,
        near,
        dilated,
        pool,
        value_weight,
        near_bias,
        near_gain,
        dilated_bias,
        far_gain,
        attn_gain,
        query_weight,
        key_weight,
    )


def solution(mesh):
    placed = (
        P(None, ("win", "seq")),
        P(None, "seq", None),
        P(),
        P(),
        P(None, "seq", None),
        P(),
        P(),
        P(None, None, "seq"),
        P(),
        P(),
        P(),
        P("seq", None),
    )

    def body(*args):
        near_weight, value_weight = args[1], args[11]
        count = lax.axis_size("seq")
        fits = (
            lax.axis_size("win") == 4
            and count % 2 == 0
            and near_weight.shape[1] % 16 == 0
            and value_weight.shape[0] % 64 == 0
            and args[0].shape[1] % 128 == 0
        )
        return fused(*args) if fits else shards(*args)

    return jax.shard_map(
        body, mesh=mesh, in_specs=placed, out_specs=P(("win", "seq"), None), check_vma=False
    )
```

```python
import functools

import jax
import jax.numpy as jnp
from jax import lax
from jax.experimental import pallas as pl
from jax.experimental.pallas import tpu as pltpu
from jax.sharding import PartitionSpec as P

HEADS = 4
KEY = 64
VAL = 192
KS = 5
DILATION_STEP = 16


def padded_2(block, sides, width):
    for axis, dim in sides:
        count = lax.axis_size(axis)
        forward = [(i, i + 1) for i in range(count - 1)]
        backward = [(target, source) for source, target in forward]
        low = lax.ppermute(
            lax.slice_in_dim(block, block.shape[dim] - width, None, axis=dim), axis, forward
        )
        high = lax.ppermute(lax.slice_in_dim(block, 0, width, axis=dim), axis, backward)
        block = jnp.concatenate([low, block, high], axis=dim)
    return block


def activate(field, gain):
    wide = field.astype(jnp.float32)
    square = jnp.mean(wide * wide, axis=0, keepdims=True)
    scaled = wide * lax.rsqrt(square + 1e-06) * gain[:, None]
    return jax.nn.gelu(scaled, approximate=False).astype(jnp.bfloat16)


def convolution_taps(padded, weight, spread):
    length = padded.shape[1] - 4 * spread
    stacked = jnp.stack([padded[:, t * spread : t * spread + length] for t in range(KS)])
    return jnp.einsum("toc,tcl->ol", weight, stacked, preferred_element_type=jnp.float32)


def attend_step(carry, pieces, queries, heads):
    running_top, running_sum, running_acc = carry
    keys, values = pieces
    count = keys.shape[0]
    key_heads = keys.reshape(count, heads, -1)
    value_heads = values.reshape(count, heads, -1)
    value_size = value_heads.shape[2]
    scores = jnp.einsum("phk,nhk->hpn", queries, key_heads, preferred_element_type=jnp.float32)
    new_top = jnp.maximum(running_top, jnp.max(scores, axis=-1))
    factor = jnp.exp(running_top - new_top)
    raised = jnp.exp(scores - new_top[:, :, None])
    new_sum = jnp.sum(raised, axis=-1)
    summed = jnp.einsum(
        "hpn,nhv->phv", raised.astype(jnp.bfloat16), value_heads, preferred_element_type=jnp.float32
    )
    widened = jnp.repeat(jnp.transpose(factor), value_size, axis=1)
    new_acc = running_acc * widened + summed.reshape(summed.shape[0], heads * value_size)
    return (new_top, new_sum, new_acc)


def shards(
    conv_input,
    near_weight,
    near_bias,
    near_gain,
    dilated_weight,
    dilated_bias,
    far_gain,
    pool_weight,
    attn_gain,
    query_weight,
    key_weight,
    value_weight,
):
    near_taps, dilated_taps, pool_taps = (
        lax.all_gather(near_weight, "seq", axis=1, tiled=True),
        lax.all_gather(dilated_weight, "seq", axis=1, tiled=True),
        lax.all_gather(pool_weight, "seq", axis=2, tiled=True),
    )
    near_act = activate(conv_input, near_gain)
    near_pad = padded_2(near_act, (("seq", 1),), 2)
    local_output = (
        conv_input.astype(jnp.float32)
        + near_bias[:, None]
        + convolution_taps(near_pad, near_taps, 1)
    ).astype(jnp.bfloat16)
    dilated_activation = activate(local_output, far_gain)
    dilated_padding = padded_2(dilated_activation, (("seq", 1),), 2 * DILATION_STEP)
    dilated_output = (
        local_output.astype(jnp.float32)
        + dilated_bias[:, None]
        + convolution_taps(dilated_padding, dilated_taps, DILATION_STEP)
    ).astype(jnp.bfloat16)
    pool_act = jax.nn.gelu(dilated_output.astype(jnp.float32), approximate=False).astype(
        jnp.bfloat16
    )
    pooled = jnp.einsum(
        "cp,cd->pd", pool_act[:, 0::2], pool_taps[0], preferred_element_type=jnp.float32
    )
    pooled = pooled + jnp.einsum(
        "cp,cd->pd", pool_act[:, 1::2], pool_taps[1], preferred_element_type=jnp.float32
    )
    square = jnp.mean(pooled * pooled, axis=1, keepdims=True)
    normed = (pooled * lax.rsqrt(square + 1e-06) * attn_gain[None, :]).astype(jnp.bfloat16)
    queries = (
        jnp.dot(normed, query_weight, preferred_element_type=jnp.float32) * KEY ** (-0.5)
    ).astype(jnp.bfloat16)
    keys = jnp.dot(normed, key_weight, preferred_element_type=jnp.float32).astype(jnp.bfloat16)
    rows = normed.shape[0]
    values = jnp.dot(
        normed,
        lax.all_gather(value_weight, "seq", axis=0, tiled=True),
        preferred_element_type=jnp.float32,
    ).astype(jnp.bfloat16)
    query_heads = queries.reshape(rows, HEADS, KEY)
    start_carry = (
        jnp.full((HEADS, rows), -1e30, jnp.float32),
        jnp.zeros((HEADS, rows), jnp.float32),
        jnp.zeros((rows, HEADS * VAL), jnp.float32),
    )
    final = attend_step(
        start_carry,
        (
            lax.all_gather(keys, "seq", axis=0, tiled=True),
            lax.all_gather(values, "seq", axis=0, tiled=True),
        ),
        query_heads,
        HEADS,
    )
    final_top, final_sum, final_acc = final
    denom = jnp.repeat(jnp.transpose(final_sum), VAL, axis=1)
    return (final_acc / denom).astype(jnp.bfloat16)

def fused_body(
    nz,
    x_ref,
    near_ref,
    dil_ref,
    pool_ref,
    val_ref,
    nb_ref,
    ng_ref,
    db_ref,
    fg_ref,
    gain_ref,
    qw_hbm,
    kw_hbm,
    out_ref,
    x_s,
    g_near,
    g_dil,
    g_pool,
    g_val,
    g_k,
    g_v,
    taps_s,
    qw_ref,
    kw_ref,
    ssem,
    rsem,
    lsem,
):
    n = 2 * nz
    w = lax.axis_index("win")
    s0 = lax.axis_index("seq")
    z = s0 // 2
    c = s0 % 2
    wx = w + 1 - 2 * (w % 2)
    wy = w + 2 - 4 * (w // 2)
    wg = wy + 1 - 2 * (w % 2)
    partner = s0 + 1 - 2 * c
    cross = s0 - 1 + 2 * c
    cross_ok = jnp.logical_and(cross >= 0, cross < n)
    local = x_ref.shape[1]
    ups = {"u": z + 1 < nz, "d": z > 0}
    steps = [(way, d) for d in range(1, nz) for way in ("u", "d")]

    def exists(way, d):
        return z >= d if way == "u" else z + d < nz

    def shard_of(way, d, core):
        return 2 * (z - d if way == "u" else z + d) + core

    def onward(way):
        return {"win": w, "seq": s0 + 2 if way == "u" else s0 - 2}

    to_x = {"win": wx, "seq": s0}
    to_y = {"win": wy, "seq": s0}
    to_c = {"win": w, "seq": partner}

    table = {}
    pending = []

    def remote(label, src, dst, device):
        index = table.setdefault(label, len(table))
        return pltpu.make_async_remote_copy(
            src_ref=src,
            dst_ref=dst,
            send_sem=ssem.at[index],
            recv_sem=rsem.at[index],
            device_id=device,
            device_id_type=pl.DeviceIdType.MESH,
        )

    def send(cond, label, src, dst, device):
        def go():
            remote(label, src(), dst(), device).start()

        def end():
            remote(label, src(), dst(), device).wait_send()

        if cond is None:
            go()
        else:
            pl.when(cond)(go)
        pending.append((cond, end))

    def receive(label, dst):
        remote(label, dst, dst, to_c).wait_recv()

    sources = {"A": near_ref, "B": dil_ref, "C": pool_ref, "D": val_ref}
    held = {"A": g_near, "B": g_dil, "C": g_pool, "D": g_val, "K": g_k, "V": g_v}
    by_x = {"A": True, "B": False, "C": True, "D": False}

    def solid(p, s):
        return held[p].at[s, pl.ds(0, sources[p].shape[0])]

    def region(p, s, q):
        rows = held[p].shape[1] // 4
        return held[p].at[s, pl.ds(pl.multiple_of(q * rows, 16), rows)]

    def local_copy(p):
        return pltpu.make_async_copy(sources[p], solid(p, s0), lsem.at["ABCD".index(p)])

    def begin(p):
        for way in ("u", "d"):
            send(
                ups[way],
                (p, "z", way, 1),
                lambda: region(p, s0, w),
                lambda: region(p, s0, w),
                onward(way),
            )

    def begin_core(p):
        send(None, (p, "c"), lambda: sources[p], lambda: solid(p, s0), to_c)

    def step1(p):
        for way, d in steps:
            s = shard_of(way, d, c)
            piece = lambda s=s: region(p, s, w)
            ok = exists(way, d)
            pl.when(ok)(lambda: receive((p, "z", way, d), piece()))
            if d + 1 < nz:
                more = jnp.logical_and(ok, ups[way])
                send(more, (p, "z", way, d + 1), piece, piece, onward(way))
            send(ok, (p, "x", way, d), piece, piece, to_x)
            send(ok, (p, "y", way, d), piece, piece, to_y)

    def step2(p):
        for way, d in steps:
            s = shard_of(way, d, c)
            ok = exists(way, d)

            @pl.when(ok)
            def _():
                receive((p, "x", way, d), region(p, s, wx))
                receive((p, "y", way, d), region(p, s, wy))

            q, device = (wy, to_x) if by_x[p] else (wx, to_y)
            piece = lambda s=s, q=q: region(p, s, q)
            send(ok, (p, "g", way, d), piece, piece, device)

    def step3(p):
        for way, d in steps:
            s = shard_of(way, d, c)
            ok = exists(way, d)
            pl.when(ok)(lambda: receive((p, "g", way, d), region(p, s, wg)))
            whole = lambda s=s: solid(p, s)
            send(ok, (p, "c", way, d), whole, whole, to_c)

    def step4(p):
        view = solid if p in sources else lambda p, s: held[p].at[s]
        receive((p, "c"), view(p, partner))
        for way, d in steps:
            s = shard_of(way, d, 1 - c)
            pl.when(exists(way, d))(lambda: receive((p, "c", way, d), view(p, s)))

    def begin_line(p):
        mine = lambda: held[p].at[s0]
        for way in ("u", "d"):
            send(ups[way], (p, "z", way, 1), mine, mine, onward(way))
        send(None, (p, "c"), mine, mine, to_c)

    def line(p):
        for way, d in steps:
            s = shard_of(way, d, c)
            whole = lambda s=s: held[p].at[s]
            ok = exists(way, d)
            pl.when(ok)(lambda: receive((p, "z", way, d), whole()))
            if d + 1 < nz:
                more = jnp.logical_and(ok, ups[way])
                send(more, (p, "z", way, d + 1), whole, whole, onward(way))
            send(ok, (p, "c", way, d), whole, whole, to_c)

    own_x = pltpu.make_async_copy(x_ref, x_s.at[:, pl.ds(128, local)], lsem.at[4])
    own_q = pltpu.make_async_copy(qw_hbm, qw_ref, lsem.at[5])
    own_k = pltpu.make_async_copy(kw_hbm, kw_ref, lsem.at[6])
    local_copy("A").start()
    own_x.start()
    for p in "BCD":
        local_copy(p).start()
    own_k.start()
    own_q.start()

    barrier = pltpu.get_barrier_semaphore()

    def greet(device):
        pl.semaphore_signal(
            barrier, inc=1, device_id=device, device_id_type=pl.DeviceIdType.MESH
        )

    for device in (to_x, to_y, to_c):
        greet(device)
    for cond, device in (
        (ups["u"], onward("u")),
        (ups["d"], onward("d")),
        (cross_ok, {"win": w, "seq": cross}),
    ):
        pl.when(cond)(lambda: greet(device))
    above, below = 1 - (z + 1) // nz, 1 - (nz - z) // nz
    pl.semaphore_wait(barrier, 3 + above + below + c * above + (1 - c) * below)

    local_copy("A").wait()
    begin("A")
    right_ok, left_ok = s0 + 1 < n, s0 > 0
    send(
        right_ok,
        "to right",
        lambda: x_ref.at[:, pl.ds(local - 128, 128)],
        lambda: x_s.at[:, pl.ds(0, 128)],
        {"win": w, "seq": s0 + 1},
    )
    send(
        left_ok,
        "to left",
        lambda: x_ref.at[:, pl.ds(0, 128)],
        lambda: x_s.at[:, pl.ds(128 + local, 128)],
        {"win": w, "seq": s0 - 1},
    )
    begin_core("A")
    for p in "BCD":
        local_copy(p).wait()
        begin(p)
        begin_core(p)
    own_x.wait()
    pl.when(left_ok)(lambda: receive("to right", x_s.at[:, pl.ds(0, 128)]))
    pl.when(right_ok)(lambda: receive("to left", x_s.at[:, pl.ds(128 + local, 128)]))

    wide = local + 128
    place = s0 * local - 64 + lax.broadcasted_iota(jnp.int32, (1, wide), 1)
    inside = jnp.logical_and(place >= 0, place < n * local)

    def act(field, gain):
        square = jnp.mean(field * field, axis=0, keepdims=True)
        scaled = field * lax.rsqrt(square + 1e-06) * gain
        return gelu(scaled)

    def conv(stack, length, weights):
        total = None
        for t in range(KS):
            taps = weights[:, pl.ds(t * rows, rows), :].reshape(channels, channels)
            term = jnp.dot(
                taps, stack[t, :, pl.ds(0, length)], preferred_element_type=jnp.float32
            )
            total = term if total is None else total + term
        return total

    channels = x_ref.shape[0]
    rows = channels // n
    diagonal = lax.broadcasted_iota(
        jnp.int32, (channels, channels), 0
    ) == lax.broadcasted_iota(jnp.int32, (channels, channels), 1)

    def column(ref):
        return jnp.sum(jnp.where(diagonal, ref[...].reshape(1, channels), 0.0), axis=1, keepdims=True)

    x = pltpu.roll(x_s[...].astype(jnp.float32), wide + 64, 1)[:, :wide]
    x = jnp.where(inside, x, 0.0)
    near_act = act(x, column(ng_ref))
    for t in range(KS):
        shift = (2 - t) % wide
        rolled = near_act if shift == 0 else pltpu.roll(near_act, shift, 1)
        taps_s[t] = rolled.astype(jnp.bfloat16)
    step1("A")
    step2("A")
    step1("B")
    step3("A")
    step2("B")
    step1("C")
    step4("A")
    near_out = (x + column(nb_ref) + conv(taps_s, wide, g_near)).astype(jnp.bfloat16)
    step3("B")
    step2("C")
    near_wide = near_out.astype(jnp.float32)
    far_act = jnp.where(inside, act(near_wide, column(fg_ref)), 0.0)
    step1("D")
    for t in range(KS):
        rolled = pltpu.roll(far_act, wide - 64 - DILATION_STEP * (t - 2), 1)
        taps_s[t, :, pl.ds(0, local)] = rolled[:, :local].astype(jnp.bfloat16)
    own_out = pltpu.roll(near_wide, wide - 64, 1)[:, :local]
    step4("B")
    step3("C")
    far_out = (own_out + column(db_ref) + conv(taps_s, local, g_dil)).astype(jnp.bfloat16)
    step2("D")
    pool_act = gelu(far_out.astype(jnp.float32)).astype(jnp.bfloat16)
    half = local // 2
    row = lax.broadcasted_iota(jnp.int32, (local, local), 0)
    col = lax.broadcasted_iota(jnp.int32, (local, local), 1)
    picker = jnp.where(row < half, 2 * row, 2 * (row - half) + 1) == col
    picked = lax.dot_general(
        picker.astype(jnp.bfloat16),
        pool_act,
        (((1,), (1,)), ((), ())),
        preferred_element_type=jnp.float32,
    ).astype(jnp.bfloat16)
    even, odd = picked[:half], picked[half:]
    step4("C")
    depth = pool_ref.shape[0] // 2
    features = n * depth

    def pool(rows_of, tap):
        taps = g_pool[:, pl.ds(tap * depth, depth), :].reshape(features, channels)
        return lax.dot_general(
            rows_of, taps, (((1,), (1,)), ((), ())), preferred_element_type=jnp.float32
        )

    pooled = pool(even, 0) + pool(odd, 1)
    square = jnp.mean(pooled * pooled, axis=1, keepdims=True)
    gain = gain_ref[...].reshape(1, features)
    normed = (pooled * lax.rsqrt(square + 1e-06) * gain).astype(jnp.bfloat16)
    own_k.wait()
    own_q.wait()

    def project(weight):
        return jnp.dot(normed, weight, preferred_element_type=jnp.float32)

    keys = project(kw_ref[...])
    g_k[s0] = keys.astype(jnp.bfloat16)
    begin_line("K")
    step3("D")
    step4("D")
    values = project(g_val[...].reshape(features, HEADS * VAL))
    g_v[s0] = values.astype(jnp.bfloat16)
    begin_line("V")
    line("K")
    queries = project(qw_ref[...]) * KEY ** (-0.5)
    queries = queries.astype(jnp.bfloat16)
    step4("K")
    lane = lax.broadcasted_iota(jnp.int32, (half, 2 * KEY), 1)
    weights, sums = [], []
    for pair in range(HEADS // 2):
        side = queries[:, pair * 2 * KEY : (pair + 1) * 2 * KEY]
        both = jnp.concatenate(
            [jnp.where(lane < KEY, side, 0.0), jnp.where(lane < KEY, 0.0, side)], axis=0
        ).astype(jnp.bfloat16)
        scores = lax.dot_general(
            both,
            g_k[:, :, pl.ds(pair * 2 * KEY, 2 * KEY)].reshape(n * half, 2 * KEY),
            (((1,), (1,)), ((), ())),
            preferred_element_type=jnp.float32,
        )
        raised = jnp.exp(scores - jnp.max(scores, axis=1, keepdims=True))
        sums.append(jnp.sum(raised, axis=1, keepdims=True))
        weights.append(raised.astype(jnp.bfloat16))
        if pair == 0:
            line("V")
    step4("V")
    lane = lax.broadcasted_iota(jnp.int32, (half, 2 * VAL), 1)
    for pair in range(HEADS // 2):
        span = pl.ds(pair * 2 * VAL, 2 * VAL)
        summed = jnp.dot(
            weights[pair],
            g_v[:, :, span].reshape(n * half, 2 * VAL),
            preferred_element_type=jnp.float32,
        )
        result = summed / sums[pair]
        out_ref[:, span] = jnp.where(lane < VAL, result[:half], result[half:]).astype(
            jnp.bfloat16
        )
    for cond, end in pending:
        if cond is None:
            end()
        else:
            pl.when(cond)(end)


def gelu(x):
    return 0.5 * x * (1.0 + lax.erf(x * 0.7071067811865476))


def fused(
    conv_input,
    near_weight,
    near_bias,
    near_gain,
    dilated_weight,
    dilated_bias,
    far_gain,
    pool_weight,
    attn_gain,
    query_weight,
    key_weight,
    value_weight,
):
    n = lax.axis_size("seq")
    nz = n // 2
    channels, local = conv_input.shape
    half = local // 2

    def flat(weight):
        return weight.reshape(weight.shape[0] * weight.shape[1], channels)

    near, dilated = flat(near_weight), flat(dilated_weight)
    pool = flat(jnp.transpose(pool_weight, (0, 2, 1)))
    any_spec = pl.BlockSpec(memory_space=pl.ANY)
    vmem = pl.BlockSpec(memory_space=pltpu.VMEM)
    count = (4 * 5 + 2 * 2) * 2 * (nz - 1) + 6 + 2
    gathered = lambda a: pltpu.VMEM((n, a.shape[0] + -a.shape[0] % 64, a.shape[1]), jnp.bfloat16)
    wide = local + 128
    return pl.pallas_call(
        functools.partial(fused_body, nz),
        out_shape=jax.ShapeDtypeStruct((half, HEADS * VAL), jnp.bfloat16),
        in_specs=[any_spec] * 5 + [vmem] * 5 + [any_spec] * 2,
        out_specs=vmem,
        scratch_shapes=[
            pltpu.VMEM((channels, local + 256), jnp.bfloat16),
            gathered(near),
            gathered(dilated),
            gathered(pool),
            gathered(value_weight),
            pltpu.VMEM((n, half, HEADS * KEY), jnp.bfloat16),
            pltpu.VMEM((n, half, HEADS * VAL), jnp.bfloat16),
            pltpu.VMEM((KS, channels, wide), jnp.bfloat16),
            pltpu.VMEM(query_weight.shape, jnp.bfloat16),
            pltpu.VMEM(key_weight.shape, jnp.bfloat16),
            pltpu.SemaphoreType.DMA((count,)),
            pltpu.SemaphoreType.DMA((count,)),
            pltpu.SemaphoreType.DMA((7,)),
        ],
        compiler_params=pltpu.CompilerParams(collective_id=0, has_side_effects=True),
    )(
        conv_input,
        near,
        dilated,
        pool,
        value_weight,
        near_bias,
        near_gain,
        dilated_bias,
        far_gain,
        attn_gain,
        query_weight,
        key_weight,
    )


def solution(mesh):
    placed = (
        P(None, ("win", "seq")),
        P(None, "seq", None),
        P(),
        P(),
        P(None, "seq", None),
        P(),
        P(),
        P(None, None, "seq"),
        P(),
        P(),
        P(),
        P("seq", None),
    )

    def body(*args):
        near_weight, value_weight = args[1], args[11]
        count = lax.axis_size("seq")
        fits = (
            lax.axis_size("win") == 4
            and count % 2 == 0
            and near_weight.shape[1] % 16 == 0
            and value_weight.shape[0] % 64 == 0
            and args[0].shape[1] % 128 == 0
        )
        return fused(*args) if fits else shards(*args)

    return jax.shard_map(
        body, mesh=mesh, in_specs=placed, out_specs=P(("win", "seq"), None), check_vma=False
    )
```
